32 devices in a mesh: dp: 4 (over y, x), row: 2 (over core), col: 4 (over z).
Axes of the slice: x: 2, y: 2, z: 4, core: 2. Of those that a mesh axis runs over, the one named last changes fastest.
Arguments:
- activations: float32 [4096, 2048], P(('dp', 'row'), 'col'), may hold values from -6 to 6
- cotangent: float32 [4096, 2048], P(('dp', 'row'), 'col'), may hold values from -6 to 6
- query_weight: bfloat16 [2048, 2048], P('col', 'row'), may hold values from -0.125 to 0.125
- key_weight: bfloat16 [2048, 1024], P('col', 'row'), may hold values from -0.125 to 0.125
- value_weight: bfloat16 [2048, 1024], P('col', 'row'), may hold values from -0.125 to 0.125
- out_weight: bfloat16 [2048, 2048], P('row', 'col'), may hold values from -0.375 to 0.375
- gate_weight: bfloat16 [2048, 6144], P('col', 'row'), may hold values from -0.125 to 0.125
- up_weight: bfloat16 [2048, 6144], P('col', 'row'), may hold values from -0.125 to 0.125
- down_weight: bfloat16 [6144, 2048], P('row', 'col'), may hold values from -0.078125 to 0.078125
- norm_attn: float32 [2048], P('col'), may hold values from 0.5 to 1.5
- norm_ffn: float32 [2048], P('col'), may hold values from 0.5 to 1.5
- gain_query: float32 [128], replicated, may hold values from 0.5 to 2.5
- gain_key: float32 [128], replicated, may hold values from 0.5 to 2.5
Outputs:
- output: float32 [4096, 2048], P(('dp', 'row'), 'col')
- grad_input: float32 [4096, 2048], P(('dp', 'row'), 'col')
- grad_query: float32 [2048, 2048], P(('col', 'dp'), 'row')
- grad_key: float32 [2048, 1024], P(('col', 'dp'), 'row')
- grad_value: float32 [2048, 1024], P(('col', 'dp'), 'row')
- grad_out: float32 [2048, 2048], P(('row', 'dp'), 'col')
- grad_gate: float32 [2048, 6144], P(('col', 'dp'), 'row')
- grad_up: float32 [2048, 6144], P(('col', 'dp'), 'row')
- grad_down: float32 [6144, 2048], P(('row', 'dp'), 'col')
- grad_norm_attn: float32 [2048], P('col')
- grad_norm_ffn: float32 [2048], P('col')
- grad_gain_query: float32 [128], replicated
- grad_gain_key: float32 [128], replicated
The draws below stay inside these ranges and needn't reach their ends.
All inputs are finite; a program needn't handle non-finite values.
Results may differ from the reference program's by a relative error of at most 0.018.
Values may be sent and summed in bfloat16 or wider, within the bound.
No kernel may reach another device: no remote copies, remote signals or barrier semaphores. Data moves between devices by JAX's collectives and lax.ppermute only.
A program may use at most 256 MiB of HBM per device.

```python
import jax
import jax.numpy as jnp
from jax import lax

D = 2048
HQ = 16
KEY_VALUE_HEADS = 8
HEAD_SIZE = 128
FF = 6144
SEQUENCE_LENGTH = 1024
TOKENS = 4096
QW = 2048
KW = 1024


def levels(key, dims, cuts, least, largest):
    level, own = 1.0, jax.random.fold_in(key, 6)
    for position, blocks in cuts:
        draws = jnp.exp(jax.random.uniform(jax.random.fold_in(own, position), (blocks,), jnp.float32, least / len(cuts), largest / len(cuts)))
        level = level * jnp.repeat(draws, dims[position] // blocks).reshape([-1 if axis == position else 1 for axis in range(len(dims))])
    return level


def bell_draw(key, shape, deviation, most, shards=(), kind=jnp.bfloat16):
    values = jax.random.normal(key, shape, jnp.float32) * deviation
    if len(shards) > 0:
        values = levels(key, shape, shards, -0.22, 0.18) * values
    return jnp.clip(values, min=-most, max=most).astype(kind)


def setup_inputs(seed: int = 0) -> dict:
    seeds = jax.random.split(jax.random.key(seed), 14)
    return {
        "activations": bell_draw(seeds[0], (TOKENS, D), 1.0, 6.0, ((0, 8), (1, 4)), jnp.float32),
        "cotangent": bell_draw(seeds[1], (TOKENS, D), 1.0, 6.0, ((0, 8), (1, 4)), jnp.float32),
        "query_weight": bell_draw(seeds[2], (D, QW), D ** -0.5, 0.125, ((0, 4), (1, 2))),
        "key_weight": bell_draw(seeds[3], (D, KW), D ** -0.5, 0.125, ((0, 4), (1, 2))),
        "value_weight": bell_draw(seeds[4], (D, KW), D ** -0.5, 0.125, ((0, 4), (1, 2))),
        "out_weight": bell_draw(seeds[5], (QW, D), (QW // 8) ** -0.5, 0.375, ((0, 2), (1, 4))),
        "gate_weight": bell_draw(seeds[6], (D, FF), D ** -0.5, 0.125, ((0, 4), (1, 2))),
        "up_weight": bell_draw(seeds[7], (D, FF), D ** -0.5, 0.125, ((0, 4), (1, 2))),
        "down_weight": bell_draw(seeds[8], (FF, D), FF ** -0.5, 0.078125, ((0, 2), (1, 4))),
        "norm_attn": jnp.clip(1.0 + 0.1 * jax.random.normal(seeds[9], (D,), jnp.float32), 0.5, 1.5),
        "norm_ffn": jnp.clip(1.0 + 0.1 * jax.random.normal(seeds[10], (D,), jnp.float32), 0.5, 1.5),
        "gain_query": jnp.clip(jax.random.uniform(seeds[11], (HEAD_SIZE,), jnp.float32, 0.5, 2.5), 0.5, 2.5),
        "gain_key": jnp.clip(jax.random.uniform(seeds[12], (HEAD_SIZE,), jnp.float32, 0.5, 2.5), 0.5, 2.5),
    }


epsilon = 1e-06
rope_base = 1000000.0
masked_score = -1e+30

def rope_tables(length, head_dim):
    half_width = head_dim // 2
    frequency = rope_base ** (-(jnp.arange(half_width, dtype=jnp.float32) * 2.0) / head_dim)
    angles = jnp.arange(length, dtype=jnp.float32)[:, None] * frequency[None, :]
    angles = jnp.concatenate([angles, angles], axis=1)
    return (jnp.cos(angles), jnp.sin(angles))

def rotate(values):
    half_width = values.shape[-1] // 2
    return jnp.concatenate([-values[..., half_width:], values[..., :half_width]], axis=-1)

def unrotate(values):
    half_width = values.shape[-1] // 2
    return jnp.concatenate([values[..., half_width:], -values[..., :half_width]], axis=-1)

def head_norm(values, norm_gain):
    factor = lax.rsqrt(lax.optimization_barrier(jnp.mean(values * values, axis=-1, keepdims=True)) + epsilon)
    return (values * factor * norm_gain, factor)

def head_norm_back(values, factor, norm_gain, upstream):
    weighted = upstream * norm_gain
    inner_mean = lax.optimization_barrier(jnp.mean(weighted * values, axis=-1, keepdims=True))
    result = factor * weighted - values * factor ** 3 * inner_mean
    dgain = lax.optimization_barrier(jnp.sum((upstream * values * factor).reshape(-1, values.shape[-1]), axis=0))
    return (result, dgain)

def attend(query_rot, key_rot, value_reduced):
    length = query_rot.shape[0]
    kv_heads = key_rot.shape[1]
    head_dim = query_rot.shape[-1]
    grouped = query_rot.reshape(length, kv_heads, -1, head_dim).astype(jnp.float32)
    scores = jnp.einsum('qngd,knd->ngqk', grouped, key_rot.astype(jnp.float32)) * head_dim ** (-0.5)
    causal = jnp.arange(length)[:, None] >= jnp.arange(length)[None, :]
    scores = jnp.where(causal, scores, masked_score)
    row_peak = lax.optimization_barrier(jnp.max(scores, axis=-1, keepdims=True))
    log_total = row_peak + jnp.log(lax.optimization_barrier(jnp.sum(jnp.exp(scores - row_peak), axis=-1, keepdims=True)))
    probability = jnp.exp(scores - log_total).astype(jnp.bfloat16)
    attended = jnp.einsum('ngqk,knd->qngd', probability.astype(jnp.float32), value_reduced.astype(jnp.float32))
    return (attended.astype(jnp.bfloat16).reshape(length, -1), log_total)

def attend_back(query_rot, key_rot, value_reduced, log_total, d_attended):
    length = query_rot.shape[0]
    kv_heads = key_rot.shape[1]
    head_dim = query_rot.shape[-1]
    factor = head_dim ** (-0.5)
    grouped = query_rot.reshape(length, kv_heads, -1, head_dim).astype(jnp.float32)
    key_wide = key_rot.astype(jnp.float32)
    value_wide = value_reduced.astype(jnp.float32)
    d_grouped = d_attended.reshape(length, kv_heads, -1, head_dim).astype(jnp.float32)
    scores = jnp.einsum('qngd,knd->ngqk', grouped, key_wide) * factor
    causal = jnp.arange(length)[:, None] >= jnp.arange(length)[None, :]
    scores = jnp.where(causal, scores, masked_score)
    probability = jnp.exp(scores - log_total)
    d_prob = jnp.einsum('qngd,knd->ngqk', d_grouped, value_wide)
    d_scores = (probability * (d_prob - lax.optimization_barrier(jnp.sum(probability * d_prob, axis=-1, keepdims=True)))).astype(jnp.bfloat16).astype(jnp.float32)
    d_query = jnp.einsum('ngqk,knd->qngd', d_scores, key_wide) * factor
    d_key = jnp.einsum('ngqk,qngd->knd', d_scores, grouped) * factor
    prob_low = probability.astype(jnp.bfloat16).astype(jnp.float32)
    d_value = jnp.einsum('ngqk,qngd->knd', prob_low, d_grouped)
    return (d_query.reshape(length, -1, head_dim), d_key, d_value)

def one_sequence(seq_input, seq_cotangent, params):
    query_weight, key_weight, value_weight, out_weight, gate_weight, up_weight, down_weight, norm_attn, norm_ffn, gain_query, gain_key = params
    cosine, sine = rope_tables(SEQUENCE_LENGTH, HEAD_SIZE)
    cos_heads = cosine[:, None, :]
    sin_heads = sine[:, None, :]
    normed_attn, scale_attn = head_norm(seq_input, norm_attn)
    normed_low = normed_attn.astype(jnp.bfloat16)
    query_raw = jnp.dot(normed_low, query_weight, preferred_element_type=jnp.float32)
    key_unnormed = jnp.dot(normed_low, key_weight, preferred_element_type=jnp.float32)
    value_projected = jnp.dot(normed_low, value_weight, preferred_element_type=jnp.float32)
    query_heads = query_raw.reshape(SEQUENCE_LENGTH, HQ, HEAD_SIZE)
    key_head_rows = key_unnormed.reshape(SEQUENCE_LENGTH, KEY_VALUE_HEADS, HEAD_SIZE)
    query_normed, query_scale = head_norm(query_heads, gain_query)
    key_normed, key_scale = head_norm(key_head_rows, gain_key)
    query_rot = (query_normed * cos_heads + rotate(query_normed) * sin_heads).astype(jnp.bfloat16)
    key_rot = (key_normed * cos_heads + rotate(key_normed) * sin_heads).astype(jnp.bfloat16)
    value_reduced = value_projected.reshape(SEQUENCE_LENGTH, KEY_VALUE_HEADS, HEAD_SIZE).astype(jnp.bfloat16)
    attended, log_total = attend(query_rot, key_rot, value_reduced)
    residual = seq_input + jnp.dot(attended, out_weight, preferred_element_type=jnp.float32)
    normed_ffn, scale_ffn = head_norm(residual, norm_ffn)
    ffn_low = normed_ffn.astype(jnp.bfloat16)
    gate_raw = jnp.dot(ffn_low, gate_weight, preferred_element_type=jnp.float32)
    up_raw = jnp.dot(ffn_low, up_weight, preferred_element_type=jnp.float32)
    sigmoid_gate = jax.nn.sigmoid(gate_raw)
    hidden = (gate_raw * sigmoid_gate * up_raw).astype(jnp.bfloat16)
    output = residual + jnp.dot(hidden, down_weight, preferred_element_type=jnp.float32)
    cotangent_low = seq_cotangent.astype(jnp.bfloat16)
    grad_down = jnp.dot(hidden.T, cotangent_low, preferred_element_type=jnp.float32)
    d_hidden = jnp.dot(cotangent_low, down_weight.T, preferred_element_type=jnp.float32)
    d_gate = (d_hidden * up_raw * sigmoid_gate * (1.0 + gate_raw * (1.0 - sigmoid_gate))).astype(jnp.bfloat16)
    d_up = (d_hidden * gate_raw * sigmoid_gate).astype(jnp.bfloat16)
    grad_gate = jnp.dot(ffn_low.T, d_gate, preferred_element_type=jnp.float32)
    grad_up = jnp.dot(ffn_low.T, d_up, preferred_element_type=jnp.float32)
    d_normed_ffn = jnp.dot(d_gate, gate_weight.T, preferred_element_type=jnp.float32) + jnp.dot(d_up, up_weight.T, preferred_element_type=jnp.float32)
    d_residual_norm, dgain_ffn = head_norm_back(residual, scale_ffn, norm_ffn, d_normed_ffn)
    d_residual = seq_cotangent + d_residual_norm
    residual_low = d_residual.astype(jnp.bfloat16)
    grad_out = jnp.dot(attended.T, residual_low, preferred_element_type=jnp.float32)
    d_attended = jnp.dot(residual_low, out_weight.T, preferred_element_type=jnp.float32).astype(jnp.bfloat16)
    d_query_rot, d_key_rot, d_value = attend_back(query_rot, key_rot, value_reduced, log_total, d_attended)
    d_query_normed = d_query_rot * cos_heads + unrotate(d_query_rot * sin_heads)
    d_key_normed = d_key_rot * cos_heads + unrotate(d_key_rot * sin_heads)
    d_query, dgain_query = head_norm_back(query_heads, query_scale, gain_query, d_query_normed)
    d_key, dgain_key = head_norm_back(key_head_rows, key_scale, gain_key, d_key_normed)
    query_back = d_query.reshape(SEQUENCE_LENGTH, -1).astype(jnp.bfloat16)
    key_back = d_key.reshape(SEQUENCE_LENGTH, -1).astype(jnp.bfloat16)
    value_back = d_value.reshape(SEQUENCE_LENGTH, -1).astype(jnp.bfloat16)
    grad_query = jnp.dot(normed_low.T, query_back, preferred_element_type=jnp.float32)
    grad_key = jnp.dot(normed_low.T, key_back, preferred_element_type=jnp.float32)
    grad_value = jnp.dot(normed_low.T, value_back, preferred_element_type=jnp.float32)
    d_normed_attn = jnp.dot(query_back, query_weight.T, preferred_element_type=jnp.float32) + jnp.dot(key_back, key_weight.T, preferred_element_type=jnp.float32) + jnp.dot(value_back, value_weight.T, preferred_element_type=jnp.float32)
    d_input_norm, dgain_attn = head_norm_back(seq_input, scale_attn, norm_attn, d_normed_attn)
    grad_input = d_residual + d_input_norm
    grads = (grad_query, grad_key, grad_value, grad_out, grad_gate, grad_up, grad_down, dgain_attn, dgain_ffn, dgain_query, dgain_key)
    return (output, grad_input, grads)

def reference(activations, cotangent, query_weight, key_weight, value_weight, out_weight, gate_weight, up_weight, down_weight, norm_attn, norm_ffn, gain_query, gain_key):
    params = (query_weight, key_weight, value_weight, out_weight, gate_weight, up_weight, down_weight, norm_attn, norm_ffn, gain_query, gain_key)
    seq_total = activations.shape[0] // SEQUENCE_LENGTH
    inputs_seq = activations.reshape(seq_total, SEQUENCE_LENGTH, -1)
    cot_seq = cotangent.reshape(seq_total, SEQUENCE_LENGTH, -1)
    running = jax.tree.map(lambda array: jnp.zeros(array.shape, jnp.float32), params)

    def scan_step(totals, bundle):
        output, grad_input, grads = one_sequence(bundle[0], bundle[1], params)
        return (jax.tree.map(lambda left, right: left + right, totals, grads), (output, grad_input))
    totals, stacked = lax.scan(scan_step, running, (inputs_seq, cot_seq))
    output = stacked[0].reshape(activations.shape)
    grad_input = stacked[1].reshape(activations.shape)
    return (output, grad_input, totals[0], totals[1], totals[2], totals[3], totals[4], totals[5], totals[6], totals[7], totals[8], totals[9], totals[10])
```

```python
import jax
import jax.numpy as jnp
from jax import lax
from jax.sharding import PartitionSpec as P

HEAD_SIZE = 128
SEQUENCE_LENGTH = 1024

epsilon = 1e-06
rope_base = 1000000.0
masked_score = -1e30
low = jnp.bfloat16
wide = jnp.float32


def rope_tables(length, head_dim):
    half_width = head_dim // 2
    frequency = rope_base ** (-(jnp.arange(half_width, dtype=jnp.float32) * 2.0) / head_dim)
    angles = jnp.arange(length, dtype=jnp.float32)[:, None] * frequency[None, :]
    angles = jnp.concatenate([angles, angles], axis=1)
    return (jnp.cos(angles), jnp.sin(angles))


def rotate(values):
    half_width = values.shape[-1] // 2
    return jnp.concatenate([-values[..., half_width:], values[..., :half_width]], axis=-1)


def unrotate(values):
    half_width = values.shape[-1] // 2
    return jnp.concatenate([values[..., half_width:], -values[..., :half_width]], axis=-1)


def head_norm(values, norm_gain):
    factor = lax.rsqrt(jnp.mean(values * values, axis=-1, keepdims=True) + epsilon)
    return (values * factor * norm_gain, factor)


def head_norm_back(values, factor, norm_gain, upstream):
    weighted = upstream * norm_gain
    inner_mean = jnp.mean(weighted * values, axis=-1, keepdims=True)
    result = factor * weighted - values * factor**3 * inner_mean
    dgain = jnp.sum((upstream * values * factor).reshape(-1, values.shape[-1]), axis=0)
    return (result, dgain)


def matmul(left, right):
    return jnp.dot(left, right, preferred_element_type=wide)


def matmul_nt(left, right):
    return lax.dot_general(left, right, (((1,), (1,)), ((), ())), preferred_element_type=wide)


def matmul_tn(left, right):
    return lax.dot_general(left, right, (((0,), (0,)), ((), ())), preferred_element_type=wide)


def take(array, index, count, axis):
    return lax.dynamic_slice_in_dim(array, index * count, count, axis)


class Links:
    def __init__(self):
        self.cols = lax.axis_size("col")
        self.dps = lax.axis_size("dp")
        self.rows = lax.axis_size("row")
        self.col = lax.axis_index("col")
        self.dp = lax.axis_index("dp")
        self.row = lax.axis_index("row")

    def shift(self, array, step):
        n = self.cols
        return lax.ppermute(array, "col", [(k, (k + step) % n) for k in range(n)])

    def cross(self, array, mask):
        return lax.ppermute(array, "dp", [(k, k ^ mask) for k in range(self.dps)])

    def swap(self, array):
        return lax.ppermute(array, "row", [(0, 1), (1, 0)])

    def col_gather(self, array):
        n = self.cols
        right, left = [array], [array]
        for _ in range(n - 1):
            right.append(lax.ppermute(right[-1], "col", [(k, k + 1) for k in range(n - 1)]))
            left.append(lax.ppermute(left[-1], "col", [(k + 1, k) for k in range(n - 1)]))
        return [array] + [
            jnp.where(self.col >= s, right[s], left[n - s]) for s in range(1, n)
        ]

    def col_scatter(self, blocks):
        total = blocks[0]
        for s in range(1, self.cols):
            total = total + self.shift(blocks[s].astype(low), -s).astype(wide)
        return total

    def col_sum(self, array):
        total = array
        for s in range(1, self.cols):
            total = total + self.shift(array, s)
        return total

    def row_gather(self, own):
        other = self.swap(own)
        first = self.row == 0
        return jnp.concatenate([jnp.where(first, own, other), jnp.where(first, other, own)], axis=0)

    def row_scatter(self, array):
        half = array.shape[0] // 2
        kept = take(array, self.row, half, 0)
        sent = take(array, 1 - self.row, half, 0).astype(low)
        return kept + self.swap(sent).astype(wide)

    def dp_order(self, array, axis):
        width = array.shape[axis] // self.dps
        return jnp.concatenate(
            [take(array, self.dp ^ d, width, axis) for d in range(self.dps)], axis=axis
        )

    def dp_gather(self, array):
        return [array] + [self.cross(array, d) for d in range(1, self.dps)]

    def dp_scatter(self, blocks):
        total = blocks[0]
        for d in range(1, self.dps):
            total = total + self.cross(blocks[d].astype(low), d).astype(wide)
        return total

    def dp_sum(self, array):
        total = array
        for d in range(1, self.dps):
            total = total + self.cross(array, d)
        return total

    def col_exchange_out(self, pieces):
        n = self.cols
        return [pieces(self.col)] + [
            self.shift(pieces((self.col + s) % n), s) for s in range(1, n)
        ]

    def widen_columns(self, parts):
        blocks = self.col_exchange_out(parts)
        stacked = jnp.stack(blocks)
        gathered = self.dp_gather(stacked)
        joined = jnp.stack(gathered, axis=1)
        return joined.reshape(-1, joined.shape[-1])

    def narrow_columns(self, grad):
        shaped = grad.reshape(self.cols, self.dps, -1, grad.shape[-1])
        summed = self.dp_scatter([shaped[:, d] for d in range(self.dps)]).astype(low)
        return [summed[0]] + [self.shift(summed[s], -s) for s in range(1, self.cols)]

    def place_cols(self, blocks):
        stacked = jnp.stack(blocks)
        return jnp.stack(
            [
                lax.dynamic_index_in_dim(stacked, (k - self.col) % self.cols, 0, keepdims=False)
                for k in range(self.cols)
            ]
        )


def attend(query_rot, key_rot, value_reduced):
    length = query_rot.shape[0]
    kv_heads = key_rot.shape[1]
    head_dim = query_rot.shape[-1]
    grouped = query_rot.reshape(length, kv_heads, -1, head_dim)
    scores = jnp.einsum(
        "qngd,knd->ngqk", grouped, key_rot, preferred_element_type=jnp.float32
    ) * head_dim ** (-0.5)
    causal = jnp.arange(length)[:, None] >= jnp.arange(length)[None, :]
    scores = jnp.where(causal, scores, masked_score)
    row_peak = jnp.max(scores, axis=-1, keepdims=True)
    log_total = row_peak + jnp.log(jnp.sum(jnp.exp(scores - row_peak), axis=-1, keepdims=True))
    probability = jnp.exp(scores - log_total).astype(jnp.bfloat16)
    attended = jnp.einsum(
        "ngqk,knd->qngd", probability, value_reduced, preferred_element_type=jnp.float32
    )
    return (attended.astype(jnp.bfloat16).reshape(length, -1), log_total)


def attend_back(query_rot, key_rot, value_reduced, log_total, d_attended):
    length = query_rot.shape[0]
    kv_heads = key_rot.shape[1]
    head_dim = query_rot.shape[-1]
    factor = head_dim ** (-0.5)
    grouped = query_rot.reshape(length, kv_heads, -1, head_dim)
    d_grouped = d_attended.reshape(length, kv_heads, -1, head_dim)
    scores = (
        jnp.einsum("qngd,knd->ngqk", grouped, key_rot, preferred_element_type=jnp.float32) * factor
    )
    causal = jnp.arange(length)[:, None] >= jnp.arange(length)[None, :]
    scores = jnp.where(causal, scores, masked_score)
    probability = jnp.exp(scores - log_total)
    d_prob = jnp.einsum(
        "qngd,knd->ngqk", d_grouped, value_reduced, preferred_element_type=jnp.float32
    )
    d_scores = (
        probability * (d_prob - jnp.sum(probability * d_prob, axis=-1, keepdims=True))
    ).astype(jnp.bfloat16)
    d_query = (
        jnp.einsum("ngqk,knd->qngd", d_scores, key_rot, preferred_element_type=jnp.float32) * factor
    )
    d_key = (
        jnp.einsum("ngqk,qngd->knd", d_scores, grouped, preferred_element_type=jnp.float32) * factor
    )
    d_value = jnp.einsum(
        "ngqk,qngd->knd",
        probability.astype(jnp.bfloat16),
        d_grouped,
        preferred_element_type=jnp.float32,
    )
    return (d_query.reshape(length, -1, head_dim), d_key, d_value)


def body(
    activations,
    cotangent,
    query_weight,
    key_weight,
    value_weight,
    out_weight,
    gate_weight,
    up_weight,
    down_weight,
    norm_attn,
    norm_ffn,
    gain_query,
    gain_key,
):
    links = Links()
    cols, dps = links.cols, links.dps
    local_width = activations.shape[1]
    width = local_width * cols
    ff_local = gate_weight.shape[1]
    ff_block = ff_local // cols
    ff_piece = ff_block // dps

    def own_rows(weight):
        return take(weight, links.dp, weight.shape[0] // dps, 0)

    query_own, key_own, value_own = map(own_rows, (query_weight, key_weight, value_weight))
    query_width = query_weight.shape[1] // cols
    key_width = key_weight.shape[1] // cols

    def qkv_piece(k):
        return jnp.concatenate(
            [
                take(query_own, k, query_width, 1),
                take(key_own, k, key_width, 1),
                take(value_own, k, key_width, 1),
            ],
            axis=1,
        )

    def by_col(weight):
        own = own_rows(weight)
        shaped = own.reshape(own.shape[0], dps, cols, ff_piece)
        return shaped.transpose(2, 0, 1, 3).reshape(cols, own.shape[0], ff_block)

    pair_cols = jnp.concatenate([by_col(gate_weight), by_col(up_weight)], axis=2)

    def pair_piece(k):
        return lax.dynamic_index_in_dim(pair_cols, k, 0, keepdims=False)

    down_own = take(down_weight, links.dp, ff_local // dps, 0)

    def down_piece(k):
        return take(down_own, k, ff_piece, 0)

    gains = links.dp_order(jnp.stack([norm_attn, norm_ffn]), 1)
    gains_full = jnp.concatenate(links.col_gather(gains), axis=1)
    gain_attn, gain_ffn = gains_full[0:1], gains_full[1:2]

    def full_norm(local, gain):
        blocks = links.col_gather(links.dp_order(local, 1).astype(low))
        joined = jnp.concatenate(blocks, axis=1).astype(wide)
        factor = lax.rsqrt(jnp.mean(joined * joined, axis=1, keepdims=True) + epsilon)
        normed = (joined * factor * gain).astype(low)
        return links.row_gather(normed), factor

    normed_attn, factor_attn = full_norm(activations, gain_attn)
    qkv_weight = links.widen_columns(qkv_piece)
    cotangent_low = jnp.concatenate(links.col_gather(cotangent.astype(low)), axis=1)
    cotangent_low = links.row_gather(cotangent_low)

    token_count = normed_attn.shape[0]
    seq_count = token_count // SEQUENCE_LENGTH
    cosine, sine = rope_tables(SEQUENCE_LENGTH, HEAD_SIZE)
    cos_heads = cosine[None, :, None, :]
    sin_heads = sine[None, :, None, :]

    def heads(array):
        return array.reshape(seq_count, SEQUENCE_LENGTH, -1, HEAD_SIZE)

    qkv = matmul(normed_attn, qkv_weight)
    query_heads = heads(qkv[:, :query_width])
    key_heads = heads(qkv[:, query_width : query_width + key_width])
    value_low = heads(qkv[:, query_width + key_width :]).astype(low)
    query_normed, query_scale = head_norm(query_heads, gain_query)
    key_normed, key_scale = head_norm(key_heads, gain_key)
    query_rot = (query_normed * cos_heads + rotate(query_normed) * sin_heads).astype(low)
    key_rot = (key_normed * cos_heads + rotate(key_normed) * sin_heads).astype(low)
    attended, log_total = jax.vmap(attend)(query_rot, key_rot, value_low)
    attended = attended.reshape(token_count, -1)

    attended_full = jnp.concatenate(links.col_gather(attended), axis=1)
    out_rel = jnp.concatenate(
        [take(out_weight, (links.col - s) % cols, query_width, 0) for s in range(cols)], axis=0
    )
    residual = activations + links.row_scatter(matmul(attended_full, out_rel))

    pair_weight = links.widen_columns(pair_piece)
    down_blocks = jnp.concatenate(links.col_exchange_out(down_piece), axis=1)
    down_wide = links.dp_order(jnp.concatenate(links.dp_gather(down_blocks), axis=0), 0)

    normed_ffn, factor_ffn = full_norm(residual, gain_ffn)
    pair = matmul(normed_ffn, pair_weight)
    gate_raw, up_raw = pair[:, :ff_block], pair[:, ff_block:]
    sigmoid_gate = jax.nn.sigmoid(gate_raw)
    hidden = (gate_raw * sigmoid_gate * up_raw).astype(low)

    def scatter_features(partial_sum):
        kept = links.row_scatter(partial_sum)
        return links.col_scatter(
            [kept[:, s * local_width : (s + 1) * local_width] for s in range(cols)]
        )

    d_hidden = matmul_nt(cotangent_low, down_wide)
    d_gate = (d_hidden * up_raw * sigmoid_gate * (1.0 + gate_raw * (1.0 - sigmoid_gate))).astype(low)
    d_up = (d_hidden * gate_raw * sigmoid_gate).astype(low)
    d_pair = jnp.concatenate([d_gate, d_up], axis=1)

    def norm_back(partial_sum, normed, factor, gain_local, local):
        inner = jnp.sum(partial_sum * normed.astype(wide), axis=1, keepdims=True)
        half = inner.shape[0] // 2
        kept = take(inner, links.row, half, 0) + links.swap(take(inner, 1 - links.row, half, 0))
        inner_mean = links.col_sum(kept) / width
        upstream = links.dp_order(scatter_features(partial_sum), 1)
        result = factor * (gain_local[None] * upstream) - local * (factor * factor) * inner_mean
        dgain = jnp.sum(upstream * local * factor, axis=0)
        return result, dgain

    d_residual_norm, dgain_ffn = norm_back(
        matmul_nt(d_pair, pair_weight), normed_ffn, factor_ffn, norm_ffn, residual
    )
    d_residual = cotangent + d_residual_norm
    residual_low = links.row_gather(d_residual.astype(low))
    d_attended_blocks = matmul_nt(residual_low, out_rel)
    d_attended = links.col_scatter(
        [d_attended_blocks[:, s * query_width : (s + 1) * query_width] for s in range(cols)]
    ).astype(low)

    output = residual + scatter_features(matmul(hidden, down_wide))

    grad_down_full = matmul_tn(hidden, cotangent_low)
    grad_down_sum = links.dp_scatter(
        [take(grad_down_full, links.dp ^ d, ff_piece, 0) for d in range(dps)]
    ).astype(low)
    grad_down_blocks = [grad_down_sum[:, :local_width]] + [
        links.shift(grad_down_sum[:, s * local_width : (s + 1) * local_width], -s)
        for s in range(1, cols)
    ]
    grad_down = links.place_cols(grad_down_blocks).reshape(-1, local_width).astype(wide)

    pair_blocks = links.place_cols(links.narrow_columns(matmul_tn(normed_ffn, d_pair)))

    def natural(blocks):
        shaped = blocks.reshape(cols, blocks.shape[1], dps, ff_piece)
        return shaped.transpose(1, 2, 0, 3).reshape(blocks.shape[1], -1).astype(wide)

    grad_gate = natural(pair_blocks[:, :, :ff_block])
    grad_up = natural(pair_blocks[:, :, ff_block:])

    grad_out_rel = matmul_tn(attended_full, residual_low)
    grad_out_nat = jnp.concatenate(
        [take(grad_out_rel, (links.col - k) % cols, query_width, 0) for k in range(cols)], axis=0
    )
    grad_out = links.dp_scatter(
        [take(grad_out_nat, links.dp ^ d, grad_out_nat.shape[0] // dps, 0) for d in range(dps)]
    )

    d_query_rot, d_key_rot, d_value = jax.vmap(attend_back)(
        query_rot, key_rot, value_low, log_total, heads(d_attended)
    )
    d_query_normed = d_query_rot * cos_heads + unrotate(d_query_rot * sin_heads)
    d_key_normed = d_key_rot * cos_heads + unrotate(d_key_rot * sin_heads)
    d_query, dgain_query = head_norm_back(query_heads, query_scale, gain_query, d_query_normed)
    d_key, dgain_key = head_norm_back(key_heads, key_scale, gain_key, d_key_normed)
    d_qkv = jnp.concatenate(
        [array.reshape(token_count, -1).astype(low) for array in (d_query, d_key, d_value)], axis=1
    )
    d_input_norm, dgain_attn = norm_back(
        matmul_nt(d_qkv, qkv_weight), normed_attn, factor_attn, norm_attn, activations
    )
    grad_input = d_residual + d_input_norm

    qkv_blocks = links.narrow_columns(matmul_tn(normed_attn, d_qkv))
    qkv_placed = links.place_cols(qkv_blocks).transpose(1, 0, 2)
    rows_own = qkv_placed.shape[0]

    def columns(first, count):
        return qkv_placed[:, :, first : first + count].reshape(rows_own, -1).astype(wide)

    grad_query = columns(0, query_width)
    grad_key = columns(query_width, key_width)
    grad_value = columns(query_width + key_width, key_width)

    norm_sums = jnp.stack([dgain_attn, dgain_ffn])
    norm_sums = links.dp_sum(norm_sums + links.swap(norm_sums))
    head_sums = jnp.stack([dgain_query, dgain_key])
    head_sums = head_sums + links.swap(head_sums)
    head_sums = links.dp_sum(links.col_sum(head_sums))
    return (
        output,
        grad_input,
        grad_query,
        grad_key,
        grad_value,
        grad_out,
        grad_gate,
        grad_up,
        grad_down,
        norm_sums[0],
        norm_sums[1],
        head_sums[0],
        head_sums[1],
    )


def solution(mesh):
    in_specs = (
        P(("dp", "row"), "col"),
        P(("dp", "row"), "col"),
        P("col", "row"),
        P("col", "row"),
        P("col", "row"),
        P("row", "col"),
        P("col", "row"),
        P("col", "row"),
        P("row", "col"),
        P("col"),
        P("col"),
        P(),
        P(),
    )
    out_specs = (
        P(("dp", "row"), "col"),
        P(("dp", "row"), "col"),
        P(("col", "dp"), "row"),
        P(("col", "dp"), "row"),
        P(("col", "dp"), "row"),
        P(("row", "dp"), "col"),
        P(("col", "dp"), "row"),
        P(("col", "dp"), "row"),
        P(("row", "dp"), "col"),
        P("col"),
        P("col"),
        P(),
        P(),
    )
    return jax.shard_map(body, mesh=mesh, in_specs=in_specs, out_specs=out_specs, check_vma=False)
```
